256 devices in a mesh: dp: 128 (over y, z, x), tensor: 2 (over core).
Axes of the slice: x: 4, y: 4, z: 8, core: 2. Of those that a mesh axis runs over, the one named last changes fastest.
Arguments:
- fc_grads: bfloat16 [128, 768, 3072], P('dp', None, 'tensor')
- fc_error: bfloat16 [128, 768, 3072], P('dp', None, 'tensor'), may hold values from -4 to 4
- query: float32 [3072, 32], P('tensor'), may hold values from -0.109375 to 0.109375
- gram_inverse: float32 [32, 32], replicated
- fc_master: float32 [768, 3072], P('dp', 'tensor'), may hold values from -6 to 6
- fc_momentum: float32 [768, 3072], P('dp', 'tensor'), may hold values from -3 to 3
- vec_grads: bfloat16 [128, 5376], P('dp'), may hold values from -24 to 24
- vec_master: float32 [5376], P('dp'), may hold values from -6 to 6
- vec_momentum: float32 [5376], P('dp'), may hold values from -4 to 4
Outputs:
- new_error: bfloat16 [128, 768, 3072], P('dp', None, 'tensor')
- new_momentum: float32 [768, 3072], P('dp', 'tensor')
- new_master: float32 [768, 3072], P('dp', 'tensor')
- new_weights: bfloat16 [768, 3072], P(None, 'tensor')
- vec_new_momentum: float32 [5376], P('dp')
- vec_new_master: float32 [5376], P('dp')
- vec_weights: bfloat16 [5376], replicated
The draws below stay inside these ranges and needn't reach their ends.
All inputs are finite; a program needn't handle non-finite values.
Results may differ from the reference program's by a relative error of at most 0.0085.
Values may be sent and summed in bfloat16 or wider, within the bound.
No kernel may reach another device: no remote copies, remote signals or barrier semaphores. Data moves between devices by JAX's collectives and lax.ppermute only.
A program may use at most 64 MiB of HBM per device.

```python
import jax
import jax.numpy as jnp
from jax import lax

D = 768
FF = 3072
RANK = 32
REPLICAS = 128
VEC = 5376
N_DP = 128


def draw_fc_grads(key, part):
    common_key = jax.random.fold_in(key, 11)
    noise_key = jax.random.fold_in(key, 12)
    common = 0.2 * jax.random.normal(common_key, (D, FF), jnp.float32)
    noise = jax.random.normal(noise_key, (REPLICAS, D, FF), jnp.float32)
    return (common + noise).astype(jnp.bfloat16)


def draw_gram_inverse(key, part):
    diag_key = jax.random.fold_in(key, 21)
    off_key = jax.random.fold_in(key, 22)
    bound = 0.78 / (RANK - 1)
    diag_values = jax.random.uniform(diag_key, (RANK,), jnp.float32, 0.8, 1.2)
    off_values = jax.random.uniform(off_key, (RANK, RANK), jnp.float32, -bound, bound)
    eye_mask = jnp.eye(RANK, dtype=jnp.float32)
    matrix = off_values * (1.0 - eye_mask) + eye_mask * diag_values[None, :]
    return matrix * (10.0 * D ** (-0.5))


def raised(values, rng, source, target, parts, factor):
    owner, partner = [(jnp.arange(values.shape[dim]) // (values.shape[dim] // parts)).reshape([-1 if axis == dim else 1 for axis in range(values.ndim)]) for dim in (source, target)]
    chosen = jax.random.permutation(rng, parts)[partner]
    strong = (owner == chosen) | (owner == (partner + parts // 2) % parts)
    return jnp.where(strong, factor * values, values)


def shard_levels(own_key, dims, cuts, low, top_value):
    def one(axis_at, parts):
        steps = jax.random.uniform(jax.random.fold_in(jax.random.fold_in(own_key, 6), axis_at), (parts,), jnp.float32, low / len(cuts), top_value / len(cuts))
        return jnp.repeat(jnp.exp(steps), dims[axis_at] // parts).reshape((-1,) + (1,) * (len(dims) - axis_at - 1))

    loudness = one(*cuts[0])
    for cut in cuts[1:]:
        loudness = loudness * one(*cut)
    return loudness


def scatter_about(rng, shape, deviation, most, shards=(), held_as=jnp.bfloat16):
    entries = jax.random.normal(rng, shape, jnp.float32) * deviation
    if len(shards) > 0:
        entries = shard_levels(rng, shape, shards, -0.22, 0.18) * entries
    return jnp.clip(entries, min=-most, max=most).astype(held_as)


def bell_draw_with(key, dims, deviation, most, pieces, heavy, held_as=jnp.bfloat16):
    entries = deviation * jax.random.normal(key, dims, jnp.float32)
    if pieces:
        entries = entries * shard_levels(key, dims, pieces, -0.22, 0.18)
    return jnp.clip(raised(entries, jax.random.fold_in(key, 3), *heavy), -most, most).astype(held_as)


def setup_inputs(seed: int = 0) -> dict:
    arg_keys = jax.random.split(jax.random.key(seed), 10)
    return {
        "fc_grads": draw_fc_grads(jax.random.fold_in(arg_keys[9], 71), 0),
        "fc_error": scatter_about(arg_keys[1], (REPLICAS, D, FF), 0.3, 4.0, ((0, 128), (2, 2))),
        "query": scatter_about(arg_keys[2], (FF, RANK), FF ** -0.5, 0.109375, ((0, 2),), jnp.float32),
        "gram_inverse": draw_gram_inverse(jax.random.fold_in(arg_keys[9], 71), 0),
        "fc_master": scatter_about(arg_keys[4], (D, FF), 0.5, 6.0, ((0, 128), (1, 2)), jnp.float32),
        "fc_momentum": scatter_about(arg_keys[5], (D, FF), 0.2, 3.0, ((0, 128), (1, 2)), jnp.float32),
        "vec_grads": bell_draw_with(arg_keys[6], (REPLICAS, VEC), 1.0, 24.0, ((0, 128),), (0, 1, 128, 5.5)),
        "vec_master": scatter_about(arg_keys[7], (VEC,), 0.5, 6.0, ((0, 128),), jnp.float32),
        "vec_momentum": scatter_about(arg_keys[8], (VEC,), 0.3, 4.0, ((0, 128),), jnp.float32),
    }


momentum_decay = 0.9
step_size = 0.5


def combine(grad_piece, error_piece):
    return (grad_piece.astype(jnp.float32) + error_piece.astype(jnp.float32)).astype(jnp.bfloat16)


def reference(fc_grads, fc_error, query, gram_inverse, fc_master, fc_momentum, vec_grads, vec_master, vec_momentum):
    query_b = query.astype(jnp.bfloat16)

    def row_step(total, pair):
        merged = combine(pair[0], pair[1])
        return total + jnp.dot(merged, query_b, preferred_element_type=jnp.float32), None

    row_total, unused = lax.scan(row_step, jnp.zeros((D, RANK), jnp.float32), (fc_grads, fc_error))
    row_mean = row_total / N_DP
    row_basis = jnp.dot(row_mean, gram_inverse, precision=lax.Precision.HIGHEST)
    basis_b = row_basis.astype(jnp.bfloat16)

    def col_step(total, pair):
        merged = combine(pair[0], pair[1])
        term = lax.dot_general(merged, basis_b, (((0,), (0,)), ((), ())), preferred_element_type=jnp.float32)
        return total + term, None

    col_total, unused = lax.scan(col_step, jnp.zeros((FF, RANK), jnp.float32), (fc_grads, fc_error))
    col_mean = col_total / N_DP
    approx = jnp.dot(row_basis, col_mean.T, precision=lax.Precision.HIGHEST)

    def error_step(pair):
        merged = lax.optimization_barrier(combine(pair[0], pair[1]))
        return (merged.astype(jnp.float32) - approx).astype(jnp.bfloat16)

    new_error = lax.map(error_step, (fc_grads, fc_error))
    new_momentum = momentum_decay * fc_momentum + approx
    new_master = fc_master - step_size * (approx + momentum_decay * new_momentum)
    new_weights = new_master.astype(jnp.bfloat16)
    vec_mean = jnp.sum(vec_grads.astype(jnp.float32), axis=0) / N_DP
    vec_new_momentum = momentum_decay * vec_momentum + vec_mean
    vec_new_master = vec_master - step_size * (vec_mean + momentum_decay * vec_new_momentum)
    vec_weights = vec_new_master.astype(jnp.bfloat16)
    return (new_error, new_momentum, new_master, new_weights, vec_new_momentum, vec_new_master, vec_weights)
```

```python
import jax
import jax.numpy as jnp
from jax import lax
from jax.sharding import Mesh, PartitionSpec as P

momentum_decay = 0.9
step_size = 0.5
SIZES = {"y": 4, "z": 8, "x": 4, "c": 2}
LANES = 128


def exchange(value, axis):
    n = SIZES[axis]
    return [value] + [lax.ppermute(value, axis, [(i, i ^ d) for i in range(n)]) for d in range(1, n)]


def in_order(blocks, index):
    bit = 1
    while bit < len(blocks):
        swap = (index & bit) != 0
        blocks = [jnp.where(swap, blocks[j ^ bit], blocks[j]) for j in range(len(blocks))]
        bit *= 2
    return blocks


def total(blocks):
    while len(blocks) > 1:
        blocks = [blocks[j] + blocks[j + 1] for j in range(0, len(blocks), 2)]
    return blocks[0]


def on_device(
    fc_grads,
    fc_error,
    query,
    gram_inverse,
    fc_master,
    fc_momentum,
    vec_grads,
    vec_master,
    vec_momentum,
):
    x, y, z, c = (lax.axis_index(a) for a in "xyzc")
    replica_index = (y * SIZES["z"] + z) * SIZES["x"] + x
    replicas = SIZES["y"] * SIZES["z"] * SIZES["x"]
    merged = (fc_grads[0].astype(jnp.float32) + fc_error[0].astype(jnp.float32)).astype(
        jnp.bfloat16
    )
    query_b = query.astype(jnp.bfloat16)
    row_part = lax.dot_general(
        query_b, merged, (((0,), (1,)), ((), ())), preferred_element_type=jnp.float32
    )
    rank, width = row_part.shape
    half = rank // 2
    row_half = lax.dynamic_slice_in_dim(row_part, c * half, half, 0)
    row_other = lax.dynamic_slice_in_dim(row_part, (1 - c) * half, half, 0)
    row_half = row_half + lax.ppermute(row_other, "c", [(0, 1), (1, 0)])

    vec_len = vec_grads.shape[1]
    shard_len = vec_master.shape[0]
    vec_half = lax.dynamic_slice_in_dim(
        vec_grads[0].astype(jnp.float32), c * (vec_len // 2), vec_len // 2, 0
    )
    vec_base = lax.dynamic_update_slice_in_dim(
        jnp.zeros((vec_len,), jnp.float32),
        vec_master - step_size * momentum_decay * momentum_decay * vec_momentum,
        replica_index * shard_len,
        0,
    )
    vec_base = lax.dynamic_slice_in_dim(vec_base, c * (vec_len // 2), vec_len // 2, 0)
    base = fc_master - step_size * momentum_decay * momentum_decay * fc_momentum

    sums = jnp.concatenate([v.reshape(-1, LANES) for v in (row_half, vec_half, vec_base)], 0)
    n_sums = sums.shape[0]
    base = base.reshape(-1, LANES)
    for axis, index in (("x", x), ("y", y)):
        blocks = exchange(jnp.concatenate([sums, base], 0), axis)
        sums = total([b[:n_sums] for b in blocks])
        base = jnp.concatenate(in_order([b[n_sums:] for b in blocks], index), 0)
    base_all = lax.all_gather(base, "z", axis=0)
    sums = total(exchange(sums, "z"))
    sums = in_order(exchange(sums, "c"), c)
    n_row = half * width // LANES
    n_vec = vec_len // 2 // LANES
    row_total = jnp.concatenate([s[:n_row].reshape(half, width) for s in sums], 0)
    vec_total = jnp.concatenate([s[n_row : n_row + n_vec].reshape(-1) for s in sums], 0)
    vec_base = jnp.concatenate([s[n_row + n_vec :].reshape(-1) for s in sums], 0)

    row_basis = lax.dot_general(
        gram_inverse,
        row_total / replicas,
        (((0,), (0,)), ((), ())),
        precision=lax.Precision.HIGHEST,
    )
    basis_b = row_basis.astype(jnp.bfloat16)
    col_part = jnp.dot(basis_b, merged, preferred_element_type=jnp.float32)
    cols = col_part.shape[1]
    plane = SIZES["z"] * SIZES["x"]
    pieces = col_part.reshape(plane, -1, LANES)
    pieces = lax.all_to_all(pieces, ("z", "x"), 0, 0, tiled=True)
    piece = total(exchange(jnp.sum(pieces, 0), "y"))
    pieces = jnp.broadcast_to(piece[None], (plane,) + piece.shape)
    pieces = lax.all_to_all(pieces, ("z", "x"), 0, 0, tiled=True)
    col_mean = pieces.reshape(rank, cols) / replicas

    approx = lax.dot_general(
        row_basis, col_mean, (((0,), (0,)), ((), ())), precision=lax.Precision.HIGHEST
    )
    new_error = (merged.astype(jnp.float32) - approx).astype(jnp.bfloat16)[None]
    gain = step_size * (1.0 + momentum_decay)
    ny, nz = SIZES["y"], SIZES["z"]
    base_all = base_all.reshape(nz, ny, -1, cols).swapaxes(0, 1).reshape(width, cols)
    new_weights = (base_all - gain * approx).astype(jnp.bfloat16)

    state_rows = fc_master.shape[0]
    basis_rows = lax.dynamic_slice_in_dim(row_basis, replica_index * state_rows, state_rows, 1)
    approx_rows = lax.dot_general(
        basis_rows, col_mean, (((0,), (0,)), ((), ())), precision=lax.Precision.HIGHEST
    )
    new_momentum = momentum_decay * fc_momentum + approx_rows
    new_master = fc_master - step_size * (approx_rows + momentum_decay * new_momentum)

    vec_total = vec_total / replicas
    vec_mean = lax.dynamic_slice_in_dim(vec_total, replica_index * shard_len, shard_len, 0)
    vec_new_momentum = momentum_decay * vec_momentum + vec_mean
    vec_new_master = vec_master - step_size * (vec_mean + momentum_decay * vec_new_momentum)
    vec_weights = (vec_base - gain * vec_total).astype(jnp.bfloat16)
    return (
        new_error,
        new_momentum,
        new_master,
        new_weights,
        vec_new_momentum,
        vec_new_master,
        vec_weights,
    )


def solution(mesh):
    grid = Mesh(mesh.devices.reshape(tuple(SIZES.values())), tuple(SIZES))
    dp = ("y", "z", "x")
    return jax.shard_map(
        on_device,
        mesh=grid,
        in_specs=(
            P(dp, None, "c"),
            P(dp, None, "c"),
            P("c", None),
            P(),
            P(dp, "c"),
            P(dp, "c"),
            P(dp, None),
            P(dp),
            P(dp),
        ),
        out_specs=(
            P(dp, None, "c"),
            P(dp, "c"),
            P(dp, "c"),
            P(None, "c"),
            P(dp),
            P(dp),
            P(),
        ),
        check_vma=False,
    )
```

```python
import functools

import jax
import jax.numpy as jnp
from jax import lax
from jax.experimental import pallas as pl
from jax.experimental.pallas import tpu as pltpu
from jax.sharding import Mesh, PartitionSpec as P

momentum_decay = 0.9
step_size = 0.5
gain = step_size * (1.0 + momentum_decay)
carried = step_size * momentum_decay * momentum_decay
SIZES = {"y": 4, "z": 8, "x": 4, "c": 2}
REPLICAS = SIZES["y"] * SIZES["z"] * SIZES["x"]
LANES = 128
VMEM = 20 << 20


def flips(value, axis, among=None):
    n = SIZES[axis]
    return [
        lax.ppermute(value, axis, [(i, i ^ d) for i in range(n)]) if d else value
        for d in among or range(n)
    ]


def total(blocks):
    while len(blocks) > 1:
        blocks = [blocks[j] + blocks[j + 1] for j in range(0, len(blocks), 2)]
    return blocks[0]


def merge(grads, error):
    return (grads.astype(jnp.float32) + error.astype(jnp.float32)).astype(jnp.bfloat16)


HBM = pl.BlockSpec(memory_space=pltpu.HBM)


def row_kernel(
    query_hbm, grads_hbm, error_hbm, master_hbm, momentum_hbm, merged_ref, payload_ref, other_ref,
    query, grads, error, master, momentum, sems,
):
    n_blocks = grads_hbm.shape[0] // LANES
    copies = [pltpu.make_async_copy(query_hbm, query, sems.at[0])]
    for i in range(n_blocks):
        at = pl.ds(i * LANES, LANES)
        copies.append(pltpu.make_async_copy(grads_hbm.at[at], grads.at[at], sems.at[1 + 2 * i]))
        copies.append(pltpu.make_async_copy(error_hbm.at[at], error.at[at], sems.at[2 + 2 * i]))
    copies.append(pltpu.make_async_copy(master_hbm, master, sems.at[1 + 2 * n_blocks]))
    copies.append(pltpu.make_async_copy(momentum_hbm, momentum, sems.at[2 + 2 * n_blocks]))
    for copy in copies:
        copy.start()
    copies[0].wait()
    query_b = query[...].astype(jnp.bfloat16)
    first = lax.axis_index("c") == 0
    half = query_b.shape[0] // 2
    for i in range(n_blocks):
        at = pl.ds(i * LANES, LANES)
        copies[1 + 2 * i].wait()
        copies[2 + 2 * i].wait()
        merged = merge(grads[at, :], error[at, :])
        merged_ref[at, :] = merged
        part = lax.dot_general(
            query_b, merged, (((1,), (1,)), ((), ())), preferred_element_type=jnp.float32
        )
        low, high = part[:half], part[half:]
        payload_ref[i * half : (i + 1) * half, :] = jnp.where(first, low, high)
        other_ref[i * half : (i + 1) * half, :] = jnp.where(first, high, low)
    copies[-2].wait()
    copies[-1].wait()
    base = master[...] - carried * momentum[...]
    groups = base.shape[1] // LANES
    n_sums = other_ref.shape[0]
    for r in range(base.shape[0]):
        for g in range(groups):
            row = n_sums + r * groups + g
            payload_ref[row : row + 1, :] = base[r : r + 1, g * LANES : (g + 1) * LANES]


def row_call(query_t, grads, error, master, momentum):
    rank, cols = query_t.shape
    rows = grads.shape[0]
    n_sums = rank // 2 * rows // LANES
    n_base = master.size // LANES
    return pl.pallas_call(
        row_kernel,
        in_specs=[HBM] * 5,
        out_shape=[
            jax.ShapeDtypeStruct(grads.shape, jnp.bfloat16),
            jax.ShapeDtypeStruct((n_sums + n_base, LANES), jnp.float32),
            jax.ShapeDtypeStruct((n_sums, LANES), jnp.float32),
        ],
        scratch_shapes=[
            pltpu.VMEM(query_t.shape, jnp.float32),
            pltpu.VMEM(grads.shape, jnp.bfloat16),
            pltpu.VMEM(grads.shape, jnp.bfloat16),
            pltpu.VMEM(master.shape, jnp.float32),
            pltpu.VMEM(master.shape, jnp.float32),
            pltpu.SemaphoreType.DMA((3 + 2 * (rows // LANES),)),
        ],
        compiler_params=pltpu.CompilerParams(vmem_limit_bytes=VMEM),
        name="row_sum",
    )(query_t, grads, error, master, momentum)


def pair_kernel(n_sums, own_ref, other_ref, out_ref):
    n = own_ref.shape[0] - n_sums
    out_ref[:n_sums, :] = own_ref[:n_sums, :] + other_ref[:n_sums, :]
    out_ref[n_sums : n_sums + n, :] = own_ref[n_sums:, :]
    out_ref[n_sums + n :, :] = other_ref[n_sums:, :]


def spread_kernel(n_sums, *refs):
    *blocks, out_ref = refs
    for k, term in enumerate(thirds(total([b[:n_sums, :] for b in blocks]))):
        out_ref[k * n_sums : (k + 1) * n_sums, :] = term
    n = blocks[0].shape[0] - n_sums
    for j, b in enumerate(blocks):
        first = 3 * n_sums + j * n
        out_ref[first : first + n, :] = b[n_sums:, :].astype(jnp.bfloat16)


def collect_kernel(n_sums, *refs):
    *blocks, sums_ref, base_ref = refs
    term = lambda b, k: b[k * n_sums : (k + 1) * n_sums, :].astype(jnp.float32)
    sums_ref[...] = total([term(b, 0) + (term(b, 1) + term(b, 2)) for b in blocks])
    n = blocks[0].shape[0] - 3 * n_sums
    for j, b in enumerate(blocks):
        base_ref[j * n : (j + 1) * n, :] = b[3 * n_sums :, :]


def blocks_call(kernel, blocks, n_sums, out_shape):
    return pl.pallas_call(
        functools.partial(kernel, n_sums),
        out_shape=out_shape,
        compiler_params=pltpu.CompilerParams(vmem_limit_bytes=VMEM),
        name=kernel.__name__,
    )(*blocks)


def column_kernel(own_ref, other_ref, gram_ref, merged_ref, vec_ref, basis_ref, piece_ref, basis_b):
    step = pl.program_id(0)
    groups = merged_ref.shape[1] // LANES
    half = own_ref.shape[0] // (basis_b.shape[1] // LANES)

    @pl.when(step == 0)
    def _():
        first = lax.axis_index("c") == 0
        own, other = own_ref[...], other_ref[...]
        low, high = jnp.where(first, own, other), jnp.where(first, other, own)
        rows = [
            jnp.concatenate([low[g * half : (g + 1) * half], high[g * half : (g + 1) * half]], 0)
            for g in range(basis_b.shape[1] // LANES)
        ]
        basis = lax.dot_general(
            gram_ref[...],
            jnp.concatenate(rows, 1) / REPLICAS,
            (((0,), (0,)), ((), ())),
            precision=lax.Precision.HIGHEST,
            preferred_element_type=jnp.float32,
        )
        width = basis_ref.shape[2]
        for k in range(basis_ref.shape[0]):
            basis_ref[k] = basis[:, k * width : (k + 1) * width]
        basis_b[...] = basis.astype(jnp.bfloat16)
        n_vec = vec_ref.shape[1]
        piece_ref[:, piece_ref.shape[1] - n_vec :, :] = vec_ref[...]

    part = jnp.dot(basis_b[...], merged_ref[...], preferred_element_type=jnp.float32)
    for j in range(pl.cdiv(piece_ref.shape[1] - vec_ref.shape[1], groups)):

        @pl.when(step == j)
        def _():
            for g in range(groups):
                piece_ref[:, j * groups + g, :] = part[:, g * LANES : (g + 1) * LANES]


def column_call(own, other, gram_inverse, merged, vec):
    rank = gram_inverse.shape[0]
    rows, cols = merged.shape
    block = 512
    pieces = cols // LANES + vec.shape[1]
    basis_shape = (SIZES["y"], rank, rows // SIZES["y"])
    whole = lambda *shape: pl.BlockSpec(shape, lambda j: (0,) * len(shape))
    return pl.pallas_call(
        column_kernel,
        grid=(cols // block,),
        in_specs=[
            whole(*own.shape),
            whole(*own.shape),
            whole(rank, rank),
            pl.BlockSpec((rows, block), lambda j: (0, j)),
            whole(*vec.shape),
        ],
        out_specs=[whole(*basis_shape), whole(rank, pieces, LANES)],
        scratch_shapes=[pltpu.VMEM((rank, rows), jnp.bfloat16)],
        out_shape=[
            jax.ShapeDtypeStruct(basis_shape, jnp.float32),
            jax.ShapeDtypeStruct((rank, pieces, LANES), jnp.float32),
        ],
        compiler_params=pltpu.CompilerParams(vmem_limit_bytes=VMEM),
        name="column_sum",
    )(own, other, gram_inverse, merged, vec)


def thirds(value):
    high = value.astype(jnp.bfloat16)
    rest = value - high.astype(jnp.float32)
    middle = rest.astype(jnp.bfloat16)
    return high, middle, (rest - middle.astype(jnp.float32)).astype(jnp.bfloat16)


def product(rows, cols3):
    high, middle, low = thirds(rows)
    left = jnp.concatenate([high, high, middle, high, low, middle], 0)
    return lax.dot_general(left, cols3, (((0,), (0,)), ((), ())), preferred_element_type=jnp.float32)


def apply_kernel(
    where, own_basis_ref, piece_ref, merged_ref, basis_hbm, base0, base1, base2, base3, master_hbm, momentum_hbm,
    new_error_ref, weights_ref, new_master_ref, new_momentum_ref,
    cols3, lane_rows, basis, base_blocks, master, momentum, sems,
):
    step = pl.program_id(0)
    cols = merged_ref.shape[1]
    groups = cols // LANES
    nx, ny, nz = SIZES["x"], SIZES["y"], SIZES["z"]
    shard = base0.shape[0] // (nx * nz)
    sources = (basis_hbm, base0, base1, base2, base3, master_hbm, momentum_hbm)
    targets = (basis, *[base_blocks.at[k] for k in range(ny)], master, momentum)
    copies = [pltpu.make_async_copy(s, t, sems.at[k]) for k, (s, t) in enumerate(zip(sources, targets))]

    @pl.when(step == 0)
    def _():
        for copy in copies:
            copy.start()
        col = jnp.concatenate([piece_ref[:, g, :] for g in range(groups)], 1) / REPLICAS
        high, middle, low = thirds(col)
        cols3[...] = jnp.concatenate([high, middle, high, low, high, middle], 0)
        copies[0].wait()

    for k in range(ny):

        @pl.when(step == k)
        def _():
            copies[1 + k].wait()
            for j in range(nx):
                for d in range(nz):
                    place = (where[1] ^ (d // 2) ^ (d % 2 * 6)) * nx + (where[2] ^ j)
                    source = (j * nz + d) * shard
                    lane_rows[pl.ds(pl.multiple_of(place * shard, 8), shard), :] = base_blocks[
                        k, source : source + shard, :
                    ].astype(jnp.float32)

    approx = product(basis[where[0] ^ step], cols3[...])
    new_error_ref[...] = (merged_ref[...].astype(jnp.float32) - approx).astype(jnp.bfloat16)
    for g in range(groups):
        lanes = slice(g * LANES, (g + 1) * LANES)
        value = lane_rows[pl.ds(g, merged_ref.shape[0], stride=groups), :]
        weights_ref[:, lanes] = (value - gain * approx[:, lanes]).astype(jnp.bfloat16)

    @pl.when(step == ny - 1)
    def _():
        copies[-2].wait()
        copies[-1].wait()
        rows_approx = product(own_basis_ref[...], cols3[...])
        new = momentum_decay * momentum[...] + rows_approx
        new_momentum_ref[...] = new
        new_master_ref[...] = master[...] - step_size * (rows_approx + momentum_decay * new)


def apply_call(where, row_basis, own_basis, pieces, merged, bases, master, momentum):
    _, rank, block = row_basis.shape
    rows, cols = merged.shape
    spec = pl.BlockSpec((block, cols), lambda i, s: (s[0] ^ i, 0))
    whole = lambda v: pl.BlockSpec(v.shape, lambda i, s: (0,) * v.ndim)
    return pl.pallas_call(
        apply_kernel,
        grid_spec=pltpu.PrefetchScalarGridSpec(
            num_scalar_prefetch=1,
            grid=(SIZES["y"],),
            in_specs=[whole(own_basis), whole(pieces), spec, *[HBM] * (3 + len(bases))],
            out_specs=[spec, spec, whole(master), whole(momentum)],
            scratch_shapes=[
                pltpu.VMEM((6 * rank, cols), jnp.bfloat16),
                pltpu.VMEM(bases[0].shape, jnp.float32),
                pltpu.VMEM(row_basis.shape, jnp.float32),
                pltpu.VMEM((len(bases), *bases[0].shape), jnp.bfloat16),
                pltpu.VMEM(master.shape, jnp.float32),
                pltpu.VMEM(master.shape, jnp.float32),
                pltpu.SemaphoreType.DMA((3 + len(bases),)),
            ],
        ),
        out_shape=[
            jax.ShapeDtypeStruct((rows, cols), jnp.bfloat16),
            jax.ShapeDtypeStruct((rows, cols), jnp.bfloat16),
            jax.ShapeDtypeStruct(master.shape, jnp.float32),
            jax.ShapeDtypeStruct(master.shape, jnp.float32),
        ],
        compiler_params=pltpu.CompilerParams(vmem_limit_bytes=VMEM),
        name="apply",
    )(where, own_basis, pieces, merged, row_basis, *bases, master, momentum)


def vec_rows_of(rank, replica_index, vec_grads, vec_master, vec_momentum):
    vec_base = lax.dynamic_update_slice_in_dim(
        jnp.zeros((vec_grads.shape[1],), jnp.float32),
        vec_master - carried * vec_momentum,
        replica_index * vec_master.shape[0],
        0,
    )
    vec = jnp.concatenate([vec_grads[0].astype(jnp.float32), vec_base], 0)
    vec_rows = pl.cdiv(vec.shape[0], rank * LANES)
    vec = jnp.pad(vec, (0, vec_rows * rank * LANES - vec.shape[0]))
    return vec.reshape(rank, vec_rows, LANES)


def on_device(
    fc_grads,
    fc_error,
    query,
    gram_inverse,
    fc_master,
    fc_momentum,
    vec_grads,
    vec_master,
    vec_momentum,
):
    x, y, z, c = (lax.axis_index(a) for a in "xyzc")
    replica_index = (y * SIZES["z"] + z) * SIZES["x"] + x
    grads, error = fc_grads[0], fc_error[0]
    rank = query.shape[1]

    merged, payload, row_other = row_call(query.T, grads, error, fc_master, fc_momentum)
    n_sums = row_other.shape[0]
    row_other = lax.ppermute(row_other, "c", [(0, 1), (1, 0)])
    payload = payload + jnp.pad(row_other, ((0, payload.shape[0] - n_sums), (0, 0)))
    n_base = payload.shape[0] - n_sums
    lanes = lambda rows, dtype: jax.ShapeDtypeStruct((rows, LANES), dtype)
    payload = blocks_call(
        pair_kernel, flips(payload, "z", (0, 6)), n_sums, lanes(n_sums + 2 * n_base, jnp.float32)
    )
    payload = blocks_call(
        spread_kernel,
        flips(payload, "z", (0, 1, 2, 3)),
        n_sums,
        lanes(3 * n_sums + 8 * n_base, jnp.bfloat16),
    )
    sums, base = blocks_call(
        collect_kernel,
        flips(payload, "x"),
        n_sums,
        [lanes(n_sums, jnp.float32), lanes(32 * n_base, jnp.bfloat16)],
    )
    vec = vec_rows_of(rank, replica_index, vec_grads, vec_master, vec_momentum)
    sums, vec = lax.optimization_barrier((sums, vec))
    sums = total(flips(sums, "y"))
    bases = flips(base, "y")
    own, other = flips(sums, "c")
    own, other, bases[0] = lax.optimization_barrier((own, other, bases[0]))

    vec_len = vec_grads.shape[1]
    shard_len = vec_master.shape[0]
    vec_rows = vec.shape[1]
    row_basis, pieces = column_call(own, other, gram_inverse, merged, vec)
    state_rows = fc_master.shape[0]
    own_basis = lax.dynamic_slice(
        row_basis, (y, 0, (z * SIZES["x"] + x) * state_rows), (1, rank, state_rows)
    )[0]

    pieces = lax.all_to_all(pieces, ("z", "x"), 0, 0, tiled=True)
    piece = total(flips(jnp.sum(pieces, 0), "y"))
    piece, *bases = lax.optimization_barrier((piece, *bases))
    pieces = jnp.broadcast_to(piece[None], (rank,) + piece.shape)
    pieces = lax.all_to_all(pieces, ("z", "x"), 0, 0, tiled=True)

    where = jnp.stack([y, z, x]).astype(jnp.int32)
    new_error, new_weights, new_master, new_momentum = apply_call(
        where, row_basis, own_basis, pieces, merged, bases, fc_master, fc_momentum
    )

    vec = pieces[:, -vec_rows:].reshape(-1)
    vec_total = vec[:vec_len] / REPLICAS
    vec_base = vec[vec_len : 2 * vec_len]
    vec_mean = lax.dynamic_slice_in_dim(vec_total, replica_index * shard_len, shard_len, 0)
    vec_new_momentum = momentum_decay * vec_momentum + vec_mean
    vec_new_master = vec_master - step_size * (vec_mean + momentum_decay * vec_new_momentum)
    vec_weights = (vec_base - gain * vec_total).astype(jnp.bfloat16)
    return (
        new_error[None],
        new_momentum,
        new_master,
        new_weights,
        vec_new_momentum,
        vec_new_master,
        vec_weights,
    )


def solution(mesh):
    grid = Mesh(mesh.devices.reshape(tuple(SIZES.values())), tuple(SIZES))
    dp = ("y", "z", "x")
    return jax.shard_map(
        on_device,
        mesh=grid,
        in_specs=(
            P(dp, None, "c"),
            P(dp, None, "c"),
            P("c", None),
            P(),
            P(dp, "c"),
            P(dp, "c"),
            P(dp, None),
            P(dp),
            P(dp),
        ),
        out_specs=(
            P(dp, None, "c"),
            P(dp, "c"),
            P(dp, "c"),
            P(None, "c"),
            P(dp),
            P(dp),
            P(),
        ),
        check_vma=False,
    )
```

```python
import functools

import jax
import jax.numpy as jnp
from jax import lax
from jax.experimental import pallas as pl
from jax.experimental.pallas import tpu as pltpu
from jax.sharding import Mesh, PartitionSpec as P

momentum_decay = 0.9
step_size = 0.5
gain = step_size * (1.0 + momentum_decay)
carried = step_size * momentum_decay * momentum_decay
SIZES = {"y": 4, "z": 8, "x": 4, "c": 2}
REPLICAS = SIZES["y"] * SIZES["z"] * SIZES["x"]
LANES = 128
VMEM = 20 << 20


def flips(value, axis, among=None):
    n = SIZES[axis]
    return [
        lax.ppermute(value, axis, [(i, i ^ d) for i in range(n)]) if d else value
        for d in among or range(n)
    ]


def total(blocks):
    while len(blocks) > 1:
        blocks = [blocks[j] + blocks[j + 1] for j in range(0, len(blocks), 2)]
    return blocks[0]


def merge(grads, error):
    return (grads.astype(jnp.float32) + error.astype(jnp.float32)).astype(jnp.bfloat16)


HBM = pl.BlockSpec(memory_space=pltpu.HBM)


def row_kernel(
    query_hbm, grads_hbm, error_hbm, master_hbm, momentum_hbm, merged_hbm, payload_ref, other_ref,
    query, grads, error, master, momentum, merged_blocks, sems, out_sems,
):
    n_blocks = grads_hbm.shape[0] // LANES
    copies = [pltpu.make_async_copy(query_hbm, query, sems.at[0])]
    for i in range(n_blocks):
        at = pl.ds(i * LANES, LANES)
        copies.append(pltpu.make_async_copy(grads_hbm.at[at], grads.at[at], sems.at[1 + 2 * i]))
        copies.append(pltpu.make_async_copy(error_hbm.at[at], error.at[at], sems.at[2 + 2 * i]))
    copies.append(pltpu.make_async_copy(master_hbm, master, sems.at[1 + 2 * n_blocks]))
    copies.append(pltpu.make_async_copy(momentum_hbm, momentum, sems.at[2 + 2 * n_blocks]))
    for copy in copies:
        copy.start()
    copies[0].wait()
    query_b = query[...].astype(jnp.bfloat16)
    first = lax.axis_index("c") == 0
    half = query_b.shape[0] // 2
    leaving = []
    for i in range(n_blocks):
        at = pl.ds(i * LANES, LANES)
        copies[1 + 2 * i].wait()
        copies[2 + 2 * i].wait()
        merged = merge(grads[at, :], error[at, :])
        merged_blocks[at, :] = merged
        leaving.append(pltpu.make_async_copy(merged_blocks.at[at], merged_hbm.at[at], out_sems.at[i]))
        leaving[i].start()
        part = lax.dot_general(
            query_b, merged, (((1,), (1,)), ((), ())), preferred_element_type=jnp.float32
        )
        low, high = part[:half], part[half:]
        payload_ref[i * half : (i + 1) * half, :] = jnp.where(first, low, high)
        other_ref[i * half : (i + 1) * half, :] = jnp.where(first, high, low)
    copies[-2].wait()
    copies[-1].wait()
    base = master[...] - carried * momentum[...]
    groups = base.shape[1] // LANES
    n_sums = other_ref.shape[0]
    for r in range(base.shape[0]):
        for g in range(groups):
            row = n_sums + r * groups + g
            payload_ref[row : row + 1, :] = base[r : r + 1, g * LANES : (g + 1) * LANES]
    for copy in leaving:
        copy.wait()


def row_call(query_t, grads, error, master, momentum):
    rank, cols = query_t.shape
    rows = grads.shape[0]
    n_sums = rank // 2 * rows // LANES
    n_base = master.size // LANES
    return pl.pallas_call(
        row_kernel,
        in_specs=[HBM] * 5,
        out_specs=[HBM] + [pl.BlockSpec(memory_space=pltpu.VMEM)] * 2,
        out_shape=[
            jax.ShapeDtypeStruct(grads.shape, jnp.bfloat16),
            jax.ShapeDtypeStruct((n_sums + n_base, LANES), jnp.float32),
            jax.ShapeDtypeStruct((n_sums, LANES), jnp.float32),
        ],
        scratch_shapes=[
            pltpu.VMEM(query_t.shape, jnp.float32),
            pltpu.VMEM(grads.shape, jnp.bfloat16),
            pltpu.VMEM(grads.shape, jnp.bfloat16),
            pltpu.VMEM(master.shape, jnp.float32),
            pltpu.VMEM(master.shape, jnp.float32),
            pltpu.VMEM(grads.shape, jnp.bfloat16),
            pltpu.SemaphoreType.DMA((3 + 2 * (rows // LANES),)),
            pltpu.SemaphoreType.DMA((rows // LANES,)),
        ],
        compiler_params=pltpu.CompilerParams(vmem_limit_bytes=60 << 20),
        name="row_sum",
    )(query_t, grads, error, master, momentum)


def split(value):
    high = value.astype(jnp.bfloat16)
    return high, (value - high.astype(jnp.float32)).astype(jnp.bfloat16)


def first_kernel(n_sums, own_ref, other_ref, out_ref):
    high, low = split(own_ref[:n_sums, :] + other_ref[...])
    out_ref[:n_sums, :] = high
    out_ref[n_sums : 2 * n_sums, :] = low
    out_ref[2 * n_sums :, :] = own_ref[n_sums:, :].astype(jnp.bfloat16)


def sums_of(block, n_sums):
    return block[:n_sums].astype(jnp.float32) + block[n_sums : 2 * n_sums].astype(jnp.float32)


def stage_kernel(n_sums, *refs):
    *blocks, out_ref = refs
    high, low = split(total([sums_of(b[: 2 * n_sums, :], n_sums) for b in blocks]))
    out_ref[:n_sums, :] = high
    out_ref[n_sums : 2 * n_sums, :] = low
    n = blocks[0].shape[0] - 2 * n_sums
    for j, b in enumerate(blocks):
        first = 2 * n_sums + j * n
        out_ref[first : first + n, :] = b[2 * n_sums :, :]


def join_kernel(n_sums, *refs):
    *blocks, out_ref = refs
    n = blocks[0].shape[0] - 2 * n_sums
    for j, b in enumerate(blocks):
        out_ref[j * n : (j + 1) * n, :] = b[2 * n_sums :, :]


def blocks_call(kernel, blocks, n_sums, out_shape):
    return pl.pallas_call(
        functools.partial(kernel, n_sums),
        out_shape=out_shape,
        compiler_params=pltpu.CompilerParams(vmem_limit_bytes=8 << 20),
        name=kernel.__name__,
    )(*blocks)


def column_kernel(own_ref, other_ref, gram_ref, merged_ref, vec_ref, basis_ref, piece_ref, basis_b):
    step = pl.program_id(0)
    groups = merged_ref.shape[1] // LANES
    half = own_ref.shape[0] // (basis_b.shape[1] // LANES)

    @pl.when(step == 0)
    def _():
        first = lax.axis_index("c") == 0
        own, other = own_ref[...], other_ref[...]
        low, high = jnp.where(first, own, other), jnp.where(first, other, own)
        rows = [
            jnp.concatenate([low[g * half : (g + 1) * half], high[g * half : (g + 1) * half]], 0)
            for g in range(basis_b.shape[1] // LANES)
        ]
        basis = lax.dot_general(
            gram_ref[...],
            jnp.concatenate(rows, 1) / REPLICAS,
            (((0,), (0,)), ((), ())),
            precision=lax.Precision.HIGHEST,
            preferred_element_type=jnp.float32,
        )
        width = basis_ref.shape[2]
        for k in range(basis_ref.shape[0]):
            basis_ref[k] = basis[:, k * width : (k + 1) * width]
        basis_b[...] = basis.astype(jnp.bfloat16)
        n_vec = vec_ref.shape[1]
        piece_ref[:, piece_ref.shape[1] - n_vec :, :] = vec_ref[...]

    part = jnp.dot(basis_b[...], merged_ref[...], preferred_element_type=jnp.float32)
    for j in range(pl.cdiv(piece_ref.shape[1] - vec_ref.shape[1], groups)):

        @pl.when(step == j)
        def _():
            for g in range(groups):
                piece_ref[:, j * groups + g, :] = part[:, g * LANES : (g + 1) * LANES]


def column_call(own, other, gram_inverse, merged, vec):
    rank = gram_inverse.shape[0]
    rows, cols = merged.shape
    block = 512
    pieces = cols // LANES + vec.shape[1]
    basis_shape = (SIZES["y"], rank, rows // SIZES["y"])
    whole = lambda *shape: pl.BlockSpec(shape, lambda j: (0,) * len(shape))
    return pl.pallas_call(
        column_kernel,
        grid=(cols // block,),
        in_specs=[
            whole(*own.shape),
            whole(*own.shape),
            whole(rank, rank),
            pl.BlockSpec((rows, block), lambda j: (0, j)),
            whole(*vec.shape),
        ],
        out_specs=[whole(*basis_shape), whole(rank, pieces, LANES)],
        scratch_shapes=[pltpu.VMEM((rank, rows), jnp.bfloat16)],
        out_shape=[
            jax.ShapeDtypeStruct(basis_shape, jnp.float32),
            jax.ShapeDtypeStruct((rank, pieces, LANES), jnp.float32),
        ],
        compiler_params=pltpu.CompilerParams(vmem_limit_bytes=VMEM),
        name="column_sum",
    )(own, other, gram_inverse, merged, vec)


def thirds(value):
    high = value.astype(jnp.bfloat16)
    rest = value - high.astype(jnp.float32)
    middle = rest.astype(jnp.bfloat16)
    return high, middle, (rest - middle.astype(jnp.float32)).astype(jnp.bfloat16)


def product(rows, cols3):
    high, middle, low = thirds(rows)
    left = jnp.concatenate([high, high, middle, high, low, middle], 0)
    return lax.dot_general(left, cols3, (((0,), (0,)), ((), ())), preferred_element_type=jnp.float32)


def apply_kernel(
    where, own_basis_ref, piece_ref, merged_ref, basis_hbm, base0, base1, base2, base3, master_hbm, momentum_hbm,
    new_error_ref, weights_ref, new_master_ref, new_momentum_ref,
    cols3, lane_rows, basis, base_blocks, master, momentum, sems,
):
    step = pl.program_id(0)
    cols = merged_ref.shape[1]
    groups = cols // LANES
    nx, ny, nz = SIZES["x"], SIZES["y"], SIZES["z"]
    shard = base0.shape[0] // (nx * nz)
    sources = (basis_hbm, base0, base1, base2, base3, master_hbm, momentum_hbm)
    targets = (basis, *[base_blocks.at[k] for k in range(ny)], master, momentum)
    copies = [pltpu.make_async_copy(s, t, sems.at[k]) for k, (s, t) in enumerate(zip(sources, targets))]

    @pl.when(step == 0)
    def _():
        for copy in copies:
            copy.start()
        col = jnp.concatenate([piece_ref[:, g, :] for g in range(groups)], 1) / REPLICAS
        high, middle, low = thirds(col)
        cols3[...] = jnp.concatenate([high, middle, high, low, high, middle], 0)
        copies[0].wait()

    for k in range(ny):

        @pl.when(step == k)
        def _():
            copies[1 + k].wait()
            for j in range(nx):
                for d in range(nz):
                    place = (where[1] ^ (d // 2) ^ (d % 2 * 6)) * nx + (where[2] ^ j)
                    source = (j * nz + d) * shard
                    lane_rows[pl.ds(pl.multiple_of(place * shard, 8), shard), :] = base_blocks[
                        k, source : source + shard, :
                    ].astype(jnp.float32)

    approx = product(basis[where[0] ^ step], cols3[...])
    new_error_ref[...] = (merged_ref[...].astype(jnp.float32) - approx).astype(jnp.bfloat16)
    for g in range(groups):
        lanes = slice(g * LANES, (g + 1) * LANES)
        value = lane_rows[pl.ds(g, merged_ref.shape[0], stride=groups), :]
        weights_ref[:, lanes] = (value - gain * approx[:, lanes]).astype(jnp.bfloat16)

    @pl.when(step == ny - 1)
    def _():
        copies[-2].wait()
        copies[-1].wait()
        rows_approx = product(own_basis_ref[...], cols3[...])
        new = momentum_decay * momentum[...] + rows_approx
        new_momentum_ref[...] = new
        new_master_ref[...] = master[...] - step_size * (rows_approx + momentum_decay * new)


def apply_call(where, row_basis, own_basis, pieces, merged, bases, master, momentum):
    _, rank, block = row_basis.shape
    rows, cols = merged.shape
    spec = pl.BlockSpec((block, cols), lambda i, s: (s[0] ^ i, 0))
    whole = lambda v: pl.BlockSpec(v.shape, lambda i, s: (0,) * v.ndim)
    return pl.pallas_call(
        apply_kernel,
        grid_spec=pltpu.PrefetchScalarGridSpec(
            num_scalar_prefetch=1,
            grid=(SIZES["y"],),
            in_specs=[whole(own_basis), whole(pieces), spec, *[HBM] * (3 + len(bases))],
            out_specs=[spec, spec, whole(master), whole(momentum)],
            scratch_shapes=[
                pltpu.VMEM((6 * rank, cols), jnp.bfloat16),
                pltpu.VMEM(bases[0].shape, jnp.float32),
                pltpu.VMEM(row_basis.shape, jnp.float32),
                pltpu.VMEM((len(bases), *bases[0].shape), jnp.bfloat16),
                pltpu.VMEM(master.shape, jnp.float32),
                pltpu.VMEM(master.shape, jnp.float32),
                pltpu.SemaphoreType.DMA((3 + len(bases),)),
            ],
        ),
        out_shape=[
            jax.ShapeDtypeStruct((rows, cols), jnp.bfloat16),
            jax.ShapeDtypeStruct((rows, cols), jnp.bfloat16),
            jax.ShapeDtypeStruct(master.shape, jnp.float32),
            jax.ShapeDtypeStruct(master.shape, jnp.float32),
        ],
        compiler_params=pltpu.CompilerParams(vmem_limit_bytes=60 << 20),
        name="apply",
    )(where, own_basis, pieces, merged, row_basis, *bases, master, momentum)


def vec_rows_of(rank, replica_index, vec_grads, vec_master, vec_momentum):
    vec_base = lax.dynamic_update_slice_in_dim(
        jnp.zeros((vec_grads.shape[1],), jnp.float32),
        vec_master - carried * vec_momentum,
        replica_index * vec_master.shape[0],
        0,
    )
    vec = jnp.concatenate([vec_grads[0].astype(jnp.float32), vec_base], 0)
    vec_rows = pl.cdiv(vec.shape[0], rank * LANES)
    vec = jnp.pad(vec, (0, vec_rows * rank * LANES - vec.shape[0]))
    return vec.reshape(rank, vec_rows, LANES)


def on_device(
    fc_grads,
    fc_error,
    query,
    gram_inverse,
    fc_master,
    fc_momentum,
    vec_grads,
    vec_master,
    vec_momentum,
):
    x, y, z, c = (lax.axis_index(a) for a in "xyzc")
    replica_index = (y * SIZES["z"] + z) * SIZES["x"] + x
    grads, error = fc_grads[0], fc_error[0]
    rank = query.shape[1]

    merged, payload, row_other = row_call(query.T, grads, error, fc_master, fc_momentum)
    n_sums = row_other.shape[0]
    row_other = lax.ppermute(row_other, "c", [(0, 1), (1, 0)])
    n_base = payload.shape[0] - n_sums
    lanes = lambda rows: jax.ShapeDtypeStruct((rows, LANES), jnp.bfloat16)
    payload = blocks_call(first_kernel, (payload, row_other), n_sums, lanes(2 * n_sums + n_base))
    blocks = flips(payload, "z", (0, 6))
    payload = blocks_call(stage_kernel, blocks, n_sums, lanes(2 * n_sums + 2 * n_base))
    blocks = flips(payload, "z", (0, 1, 2, 3))
    payload = blocks_call(stage_kernel, blocks, n_sums, lanes(2 * n_sums + 8 * n_base))
    blocks = flips(payload, "x")
    sums = total([sums_of(b, n_sums) for b in blocks])
    base = blocks_call(join_kernel, blocks, n_sums, lanes(32 * n_base))
    vec = vec_rows_of(rank, replica_index, vec_grads, vec_master, vec_momentum)
    sums, vec = lax.optimization_barrier((sums, vec))
    sums = total(flips(sums, "y"))
    bases = flips(base, "y")
    own, other = flips(sums, "c")
    own, other, bases[0] = lax.optimization_barrier((own, other, bases[0]))

    vec_len = vec_grads.shape[1]
    shard_len = vec_master.shape[0]
    vec_rows = vec.shape[1]
    row_basis, pieces = column_call(own, other, gram_inverse, merged, vec)
    state_rows = fc_master.shape[0]
    own_basis = lax.dynamic_slice(
        row_basis, (y, 0, (z * SIZES["x"] + x) * state_rows), (1, rank, state_rows)
    )[0]

    pieces = lax.all_to_all(pieces, ("z", "x"), 0, 0, tiled=True)
    piece, *bases = lax.optimization_barrier((jnp.sum(pieces, 0), *bases))
    piece = total(flips(piece, "y"))
    pieces = jnp.broadcast_to(piece[None], (rank,) + piece.shape)
    pieces = lax.all_to_all(pieces, ("z", "x"), 0, 0, tiled=True)

    where = jnp.stack([y, z, x]).astype(jnp.int32)
    new_error, new_weights, new_master, new_momentum = apply_call(
        where, row_basis, own_basis, pieces, merged, bases, fc_master, fc_momentum
    )

    vec = pieces[:, -vec_rows:].reshape(-1)
    vec_total = vec[:vec_len] / REPLICAS
    vec_base = vec[vec_len : 2 * vec_len]
    vec_mean = lax.dynamic_slice_in_dim(vec_total, replica_index * shard_len, shard_len, 0)
    vec_new_momentum = momentum_decay * vec_momentum + vec_mean
    vec_new_master = vec_master - step_size * (vec_mean + momentum_decay * vec_new_momentum)
    vec_weights = (vec_base - gain * vec_total).astype(jnp.bfloat16)
    return (
        new_error[None],
        new_momentum,
        new_master,
        new_weights,
        vec_new_momentum,
        vec_new_master,
        vec_weights,
    )


def solution(mesh):
    grid = Mesh(mesh.devices.reshape(tuple(SIZES.values())), tuple(SIZES))
    dp = ("y", "z", "x")
    return jax.shard_map(
        on_device,
        mesh=grid,
        in_specs=(
            P(dp, None, "c"),
            P(dp, None, "c"),
            P("c", None),
            P(),
            P(dp, "c"),
            P(dp, "c"),
            P(dp, None),
            P(dp),
            P(dp),
        ),
        out_specs=(
            P(dp, None, "c"),
            P(dp, "c"),
            P(dp, "c"),
            P(None, "c"),
            P(dp),
            P(dp),
            P(),
        ),
        check_vma=False,
    )
```

```python
import functools

import jax
import jax.numpy as jnp
from jax import lax
from jax.experimental import pallas as pl
from jax.experimental.pallas import tpu as pltpu
from jax.sharding import Mesh, PartitionSpec as P

momentum_decay = 0.9
step_size = 0.5
gain = step_size * (1.0 + momentum_decay)
carried = step_size * momentum_decay * momentum_decay
SIZES = {"y": 4, "z": 8, "x": 4, "c": 2}
REPLICAS = SIZES["y"] * SIZES["z"] * SIZES["x"]
LANES = 128
VMEM = 20 << 20


def flips(value, axis, among=None):
    n = SIZES[axis]
    return [
        lax.ppermute(value, axis, [(i, i ^ d) for i in range(n)]) if d else value
        for d in among or range(n)
    ]


def total(blocks):
    while len(blocks) > 1:
        blocks = [blocks[j] + blocks[j + 1] for j in range(0, len(blocks), 2)]
    return blocks[0]


def merge(grads, error):
    return (grads.astype(jnp.float32) + error.astype(jnp.float32)).astype(jnp.bfloat16)


HBM = pl.BlockSpec(memory_space=pltpu.HBM)


def row_kernel(
    query_hbm, grads_hbm, error_hbm, master_hbm, momentum_hbm, merged_hbm, payload_ref, other_ref,
    query, grads, error, master, momentum, merged_blocks, sems, out_sems,
):
    n_blocks = grads_hbm.shape[0] // LANES
    copies = [pltpu.make_async_copy(query_hbm, query, sems.at[0])]
    for i in range(n_blocks):
        at = pl.ds(i * LANES, LANES)
        copies.append(pltpu.make_async_copy(grads_hbm.at[at], grads.at[at], sems.at[1 + 2 * i]))
        copies.append(pltpu.make_async_copy(error_hbm.at[at], error.at[at], sems.at[2 + 2 * i]))
    copies.append(pltpu.make_async_copy(master_hbm, master, sems.at[1 + 2 * n_blocks]))
    copies.append(pltpu.make_async_copy(momentum_hbm, momentum, sems.at[2 + 2 * n_blocks]))
    for copy in copies:
        copy.start()
    copies[0].wait()
    query_b = query[...].astype(jnp.bfloat16)
    first = lax.axis_index("c") == 0
    half = query_b.shape[0] // 2
    leaving = []
    for i in range(n_blocks):
        at = pl.ds(i * LANES, LANES)
        copies[1 + 2 * i].wait()
        copies[2 + 2 * i].wait()
        merged = merge(grads[at, :], error[at, :])
        merged_blocks[at, :] = merged
        leaving.append(pltpu.make_async_copy(merged_blocks.at[at], merged_hbm.at[at], out_sems.at[i]))
        leaving[i].start()
        part = lax.dot_general(
            query_b, merged, (((1,), (1,)), ((), ())), preferred_element_type=jnp.float32
        )
        low, high = part[:half], part[half:]
        payload_ref[i * half : (i + 1) * half, :] = jnp.where(first, low, high)
        other_ref[i * half : (i + 1) * half, :] = jnp.where(first, high, low)
    copies[-2].wait()
    copies[-1].wait()
    base = master[...] - carried * momentum[...]
    groups = base.shape[1] // LANES
    n_sums = other_ref.shape[0]
    for r in range(base.shape[0]):
        for g in range(groups):
            row = n_sums + r * groups + g
            payload_ref[row : row + 1, :] = base[r : r + 1, g * LANES : (g + 1) * LANES]
    for copy in leaving:
        copy.wait()


def row_call(query_t, grads, error, master, momentum):
    rank, cols = query_t.shape
    rows = grads.shape[0]
    n_sums = rank // 2 * rows // LANES
    n_base = master.size // LANES
    return pl.pallas_call(
        row_kernel,
        in_specs=[HBM] * 5,
        out_specs=[HBM] + [pl.BlockSpec(memory_space=pltpu.VMEM)] * 2,
        out_shape=[
            jax.ShapeDtypeStruct(grads.shape, jnp.bfloat16),
            jax.ShapeDtypeStruct((n_sums + n_base, LANES), jnp.float32),
            jax.ShapeDtypeStruct((n_sums, LANES), jnp.float32),
        ],
        scratch_shapes=[
            pltpu.VMEM(query_t.shape, jnp.float32),
            pltpu.VMEM(grads.shape, jnp.bfloat16),
            pltpu.VMEM(grads.shape, jnp.bfloat16),
            pltpu.VMEM(master.shape, jnp.float32),
            pltpu.VMEM(master.shape, jnp.float32),
            pltpu.VMEM(grads.shape, jnp.bfloat16),
            pltpu.SemaphoreType.DMA((3 + 2 * (rows // LANES),)),
            pltpu.SemaphoreType.DMA((rows // LANES,)),
        ],
        compiler_params=pltpu.CompilerParams(vmem_limit_bytes=60 << 20),
        name="row_sum",
    )(query_t, grads, error, master, momentum)


def split(value):
    high = value.astype(jnp.bfloat16)
    return high, (value - high.astype(jnp.float32)).astype(jnp.bfloat16)


def first_kernel(n_sums, own_ref, other_ref, out_ref):
    high, low = split(own_ref[:n_sums, :] + other_ref[...])
    out_ref[:n_sums, :] = high
    out_ref[n_sums : 2 * n_sums, :] = low
    out_ref[2 * n_sums :, :] = own_ref[n_sums:, :].astype(jnp.bfloat16)


def sums_of(block, n_sums):
    return block[:n_sums].astype(jnp.float32) + block[n_sums : 2 * n_sums].astype(jnp.float32)


def stage_kernel(n_sums, *refs):
    *blocks, out_ref = refs
    high, low = split(total([sums_of(b[: 2 * n_sums, :], n_sums) for b in blocks]))
    out_ref[:n_sums, :] = high
    out_ref[n_sums : 2 * n_sums, :] = low
    n = blocks[0].shape[0] - 2 * n_sums
    for j, b in enumerate(blocks):
        first = 2 * n_sums + j * n
        out_ref[first : first + n, :] = b[2 * n_sums :, :]


def halves_kernel(n_sums, *refs):
    *blocks, out_ref, rest_ref = refs
    high, low = split(total([sums_of(b[: 2 * n_sums, :], n_sums) for b in blocks]))
    out_ref[:n_sums, :] = high
    out_ref[n_sums : 2 * n_sums, :] = low
    n = blocks[0].shape[0] - 2 * n_sums
    half = len(blocks) // 2
    for j, b in enumerate(blocks[:half]):
        first = 2 * n_sums + j * n
        out_ref[first : first + n, :] = b[2 * n_sums :, :]
    for j, b in enumerate(blocks[half:]):
        rest_ref[j * n : (j + 1) * n, :] = b[2 * n_sums :, :]


def join_kernel(n_sums, *refs):
    *blocks, out_ref = refs
    n = blocks[0].shape[0] - 2 * n_sums
    for j, b in enumerate(blocks):
        out_ref[j * n : (j + 1) * n, :] = b[2 * n_sums :, :]


def blocks_call(kernel, blocks, n_sums, out_shape):
    return pl.pallas_call(
        functools.partial(kernel, n_sums),
        out_shape=out_shape,
        compiler_params=pltpu.CompilerParams(vmem_limit_bytes=8 << 20),
        name=kernel.__name__,
    )(*blocks)


def repeat_kernel(*refs):
    *blocks, out_ref = refs
    out_ref[...] = jnp.broadcast_to(total([b[...] for b in blocks])[None], out_ref.shape)


def repeat_call(blocks, n):
    return pl.pallas_call(
        repeat_kernel,
        out_shape=jax.ShapeDtypeStruct((n, *blocks[0].shape), jnp.float32),
        compiler_params=pltpu.CompilerParams(vmem_limit_bytes=8 << 20),
        name="repeat",
    )(*blocks)


def column_kernel(own_ref, other_ref, gram_ref, merged_ref, vec_ref, basis_ref, piece_ref, basis_b):
    step = pl.program_id(0)
    groups = merged_ref.shape[1] // LANES
    n_vec = vec_ref.shape[0] // gram_ref.shape[0]
    half = own_ref.shape[0] // (basis_b.shape[1] // LANES)

    @pl.when(step == 0)
    def _():
        first = lax.axis_index("c") == 0
        own, other = own_ref[...], other_ref[...]
        low, high = jnp.where(first, own, other), jnp.where(first, other, own)
        rows = [
            jnp.concatenate([low[g * half : (g + 1) * half], high[g * half : (g + 1) * half]], 0)
            for g in range(basis_b.shape[1] // LANES)
        ]
        basis = lax.dot_general(
            gram_ref[...],
            jnp.concatenate(rows, 1) / REPLICAS,
            (((0,), (0,)), ((), ())),
            precision=lax.Precision.HIGHEST,
            preferred_element_type=jnp.float32,
        )
        width = basis_ref.shape[2]
        for k in range(basis_ref.shape[0]):
            basis_ref[k] = basis[:, k * width : (k + 1) * width]
        basis_b[...] = basis.astype(jnp.bfloat16)
        rank = gram_ref.shape[0]
        for k in range(n_vec):
            piece_ref[:, piece_ref.shape[1] - n_vec + k, :] = vec_ref[k * rank : (k + 1) * rank, :]

    part = jnp.dot(basis_b[...], merged_ref[...], preferred_element_type=jnp.float32)
    for j in range(pl.cdiv(piece_ref.shape[1] - n_vec, groups)):

        @pl.when(step == j)
        def _():
            for g in range(groups):
                piece_ref[:, j * groups + g, :] = part[:, g * LANES : (g + 1) * LANES]


def column_call(own, other, gram_inverse, merged, vec):
    rank = gram_inverse.shape[0]
    rows, cols = merged.shape
    block = 512
    pieces = cols // LANES + vec.shape[0] // rank
    basis_shape = (SIZES["y"], rank, rows // SIZES["y"])
    whole = lambda *shape: pl.BlockSpec(shape, lambda j: (0,) * len(shape))
    return pl.pallas_call(
        column_kernel,
        grid=(cols // block,),
        in_specs=[
            whole(*own.shape),
            whole(*own.shape),
            whole(rank, rank),
            pl.BlockSpec((rows, block), lambda j: (0, j)),
            whole(*vec.shape),
        ],
        out_specs=[whole(*basis_shape), whole(rank, pieces, LANES)],
        scratch_shapes=[pltpu.VMEM((rank, rows), jnp.bfloat16)],
        out_shape=[
            jax.ShapeDtypeStruct(basis_shape, jnp.float32),
            jax.ShapeDtypeStruct((rank, pieces, LANES), jnp.float32),
        ],
        compiler_params=pltpu.CompilerParams(vmem_limit_bytes=VMEM),
        name="column_sum",
    )(own, other, gram_inverse, merged, vec)


def thirds(value):
    high = value.astype(jnp.bfloat16)
    rest = value - high.astype(jnp.float32)
    middle = rest.astype(jnp.bfloat16)
    return high, middle, (rest - middle.astype(jnp.float32)).astype(jnp.bfloat16)


def product(rows, cols3):
    high, middle, low = thirds(rows)
    left = jnp.concatenate([high, high, middle, high, low, middle], 0)
    return lax.dot_general(left, cols3, (((0,), (0,)), ((), ())), preferred_element_type=jnp.float32)


def apply_kernel(
    where, own_basis_ref, piece_ref, merged_ref, basis_hbm, base0, base1, base2, base3,
    rest0, rest1, rest2, rest3, master_hbm, momentum_hbm,
    vec_master_ref, vec_momentum_ref,
    new_error_ref, weights_ref, new_master_ref, new_momentum_ref, vec_weights_ref, vec_new_master_ref, vec_new_momentum_ref,
    cols3, lane_rows, basis, base_blocks, master, momentum, vec, sems,
):
    step = pl.program_id(0)
    cols = merged_ref.shape[1]
    groups = cols // LANES
    nx, ny, nz = SIZES["x"], SIZES["y"], SIZES["z"]
    half = base0.shape[0]
    shard = half // (nx * nz // 2)
    part = half // nx
    moves = [(basis_hbm, basis)]
    for k, base in enumerate((base0, base1, base2, base3)):
        moves.append((base, base_blocks.at[k, pl.ds(0, half)]))
        for j, rest in enumerate((rest0, rest1, rest2, rest3)):
            moves.append((rest.at[pl.ds(k * part, part)], base_blocks.at[k, pl.ds(half + j * part, part)]))
    moves += [(master_hbm, master), (momentum_hbm, momentum)]
    copies = [pltpu.make_async_copy(s, t, sems.at[k]) for k, (s, t) in enumerate(moves)]

    @pl.when(step == 0)
    def _():
        for copy in copies:
            copy.start()
        col = jnp.concatenate([piece_ref[:, g, :] for g in range(groups)], 1) / REPLICAS
        high, middle, low = thirds(col)
        cols3[...] = jnp.concatenate([high, middle, high, low, high, middle], 0)
        copies[0].wait()

    for k in range(ny):

        @pl.when(step == k)
        def _():
            for copy in copies[1 + k * (nx + 1) : 1 + (k + 1) * (nx + 1)]:
                copy.wait()
            for j in range(nx):
                for d in range(nz):
                    place = (where[1] ^ (d // 2) ^ (d % 2 * 6)) * nx + (where[2] ^ j)
                    source = d // (nz // 2) * half + (j * (nz // 2) + d % (nz // 2)) * shard
                    lane_rows[pl.ds(pl.multiple_of(place * shard, 8), shard), :] = base_blocks[
                        k, source : source + shard, :
                    ].astype(jnp.float32)

    approx = product(basis[where[0] ^ step], cols3[...])
    new_error_ref[...] = (merged_ref[...].astype(jnp.float32) - approx).astype(jnp.bfloat16)
    for g in range(groups):
        lanes = slice(g * LANES, (g + 1) * LANES)
        value = lane_rows[pl.ds(g, merged_ref.shape[0], stride=groups), :]
        weights_ref[:, lanes] = (value - gain * approx[:, lanes]).astype(jnp.bfloat16)

    @pl.when(step == ny - 1)
    def _():
        copies[-2].wait()
        copies[-1].wait()
        rows_approx = product(own_basis_ref[...], cols3[...])
        new = momentum_decay * momentum[...] + rows_approx
        new_momentum_ref[...] = new
        new_master_ref[...] = master[...] - step_size * (rows_approx + momentum_decay * new)

        rank = piece_ref.shape[0]
        for k in range(piece_ref.shape[1] - groups):
            vec[k * rank : (k + 1) * rank, :] = piece_ref[:, groups + k, :]
        n_vec = vec_weights_ref.shape[0]
        change = gain * (vec[:n_vec, :] / REPLICAS)
        vec_weights_ref[...] = (vec[n_vec : 2 * n_vec, :] - change).astype(jnp.bfloat16)
        shard_len = vec_master_ref.shape[1]
        start = ((where[0] * nz + where[1]) * nx + where[2]) * shard_len
        row, lane = start // LANES, start % LANES
        turned = [
            pltpu.roll(jnp.broadcast_to(vec[pl.ds(row + k, 1), :], (8, LANES)), LANES - lane, 1)
            for k in range(2)
        ]
        here = lax.broadcasted_iota(jnp.int32, (8, LANES), 1) < LANES - lane
        mean = jnp.where(here, turned[0], turned[1])[:1, :shard_len] / REPLICAS
        new = momentum_decay * vec_momentum_ref[...] + mean
        vec_new_momentum_ref[...] = new
        vec_new_master_ref[...] = vec_master_ref[...] - step_size * (mean + momentum_decay * new)


def apply_call(where, row_basis, own_basis, pieces, merged, bases, master, momentum, vec_len, vec_master, vec_momentum):
    _, rank, block = row_basis.shape
    rows, cols = merged.shape
    spec = pl.BlockSpec((block, cols), lambda i, s: (s[0] ^ i, 0))
    whole = lambda v: pl.BlockSpec(v.shape, lambda i, s: (0,) * v.ndim)
    return pl.pallas_call(
        apply_kernel,
        grid_spec=pltpu.PrefetchScalarGridSpec(
            num_scalar_prefetch=1,
            grid=(SIZES["y"],),
            in_specs=[
                whole(own_basis), whole(pieces), spec, *[HBM] * (3 + len(bases)), whole(vec_master), whole(vec_master),
            ],
            out_specs=[
                spec, spec, whole(master), whole(momentum),
                pl.BlockSpec((vec_len // LANES, LANES), lambda i, s: (0, 0)), whole(vec_master), whole(vec_master),
            ],
            scratch_shapes=[
                pltpu.VMEM((6 * rank, cols), jnp.bfloat16),
                pltpu.VMEM((2 * bases[0].shape[0], LANES), jnp.float32),
                pltpu.VMEM(row_basis.shape, jnp.float32),
                pltpu.VMEM((SIZES["y"], 2 * bases[0].shape[0], LANES), jnp.bfloat16),
                pltpu.VMEM(master.shape, jnp.float32),
                pltpu.VMEM(master.shape, jnp.float32),
                pltpu.VMEM((rank * (pieces.shape[1] - cols // LANES), LANES), jnp.float32),
                pltpu.SemaphoreType.DMA((3 + SIZES["y"] * (SIZES["x"] + 1),)),
            ],
        ),
        out_shape=[
            jax.ShapeDtypeStruct((rows, cols), jnp.bfloat16),
            jax.ShapeDtypeStruct((rows, cols), jnp.bfloat16),
            jax.ShapeDtypeStruct(master.shape, jnp.float32),
            jax.ShapeDtypeStruct(master.shape, jnp.float32),
            jax.ShapeDtypeStruct((vec_len // LANES, LANES), jnp.bfloat16),
            jax.ShapeDtypeStruct(vec_master.shape, jnp.float32),
            jax.ShapeDtypeStruct(vec_master.shape, jnp.float32),
        ],
        compiler_params=pltpu.CompilerParams(vmem_limit_bytes=60 << 20),
        name="apply",
    )(where, own_basis, pieces, merged, row_basis, *bases, master, momentum, vec_master, vec_momentum)


def vec_rows_of(rank, replica_index, vec_grads, vec_master, vec_momentum):
    vec_base = lax.dynamic_update_slice_in_dim(
        jnp.zeros((vec_grads.shape[1],), jnp.float32),
        vec_master - carried * vec_momentum,
        replica_index * vec_master.shape[0],
        0,
    )
    vec = jnp.concatenate([vec_grads[0].astype(jnp.float32), vec_base], 0)
    vec_rows = pl.cdiv(vec.shape[0], rank * LANES)
    vec = jnp.pad(vec, (0, vec_rows * rank * LANES - vec.shape[0]))
    return vec.reshape(vec_rows * rank, LANES)


def on_device(
    fc_grads,
    fc_error,
    query,
    gram_inverse,
    fc_master,
    fc_momentum,
    vec_grads,
    vec_master,
    vec_momentum,
):
    x, y, z, c = (lax.axis_index(a) for a in "xyzc")
    replica_index = (y * SIZES["z"] + z) * SIZES["x"] + x
    grads, error = fc_grads[0], fc_error[0]
    rank = query.shape[1]

    merged, payload, row_other = row_call(query.T, grads, error, fc_master, fc_momentum)
    n_sums = row_other.shape[0]
    row_other = lax.ppermute(row_other, "c", [(0, 1), (1, 0)])
    n_base = payload.shape[0] - n_sums
    lanes = lambda rows: jax.ShapeDtypeStruct((rows, LANES), jnp.bfloat16)
    payload = blocks_call(first_kernel, (payload, row_other), n_sums, lanes(2 * n_sums + n_base))
    blocks = flips(payload, "z", (0, 6))
    payload = blocks_call(stage_kernel, blocks, n_sums, lanes(2 * n_sums + 2 * n_base))
    blocks = flips(payload, "z", (0, 1, 2, 3))
    payload, rest = blocks_call(
        halves_kernel, blocks, n_sums, [lanes(2 * n_sums + 4 * n_base), lanes(4 * n_base)]
    )
    blocks = flips(payload, "x")
    rests = flips(rest, "y")
    sums = total([sums_of(b, n_sums) for b in blocks])
    base = blocks_call(join_kernel, blocks, n_sums, lanes(16 * n_base))
    rest = blocks_call(join_kernel, rests, 0, lanes(16 * n_base))
    vec = vec_rows_of(rank, replica_index, vec_grads, vec_master, vec_momentum)
    sums, vec = lax.optimization_barrier((sums, vec))
    sums = total(flips(sums, "y"))
    bases = flips(base, "y") + flips(rest, "x")
    own, other = flips(sums, "c")
    own, other, bases[0], bases[4] = lax.optimization_barrier((own, other, bases[0], bases[4]))

    row_basis, pieces = column_call(own, other, gram_inverse, merged, vec)
    state_rows = fc_master.shape[0]
    own_basis = lax.dynamic_slice(
        row_basis, (y, 0, (z * SIZES["x"] + x) * state_rows), (1, rank, state_rows)
    )[0]

    near = (1, 5)
    pieces, *arrived = lax.optimization_barrier((pieces, *[bases[k] for k in near]))
    for k, block in zip(near, arrived):
        bases[k] = block
    pieces = lax.all_to_all(pieces, ("z", "x"), 0, 0, tiled=True)
    piece, *bases = lax.optimization_barrier((jnp.sum(pieces, 0), *bases))
    pieces = repeat_call(flips(piece, "y"), rank)
    pieces = lax.all_to_all(pieces, ("z", "x"), 0, 0, tiled=True)

    where = jnp.stack([y, z, x]).astype(jnp.int32)
    new_error, new_weights, new_master, new_momentum, vec_weights, vec_new_master, vec_new_momentum = apply_call(
        where, row_basis, own_basis, pieces, merged, bases, fc_master, fc_momentum,
        vec_grads.shape[1], vec_master[None], vec_momentum[None],
    )
    return (
        new_error[None],
        new_momentum,
        new_master,
        new_weights,
        vec_new_momentum[0],
        vec_new_master[0],
        vec_weights.reshape(-1),
    )


def solution(mesh):
    grid = Mesh(mesh.devices.reshape(tuple(SIZES.values())), tuple(SIZES))
    dp = ("y", "z", "x")
    return jax.shard_map(
        on_device,
        mesh=grid,
        in_specs=(
            P(dp, None, "c"),
            P(dp, None, "c"),
            P("c", None),
            P(),
            P(dp, "c"),
            P(dp, "c"),
            P(dp, None),
            P(dp),
            P(dp),
        ),
        out_specs=(
            P(dp, None, "c"),
            P(dp, "c"),
            P(dp, "c"),
            P(None, "c"),
            P(dp),
            P(dp),
            P(),
        ),
        check_vma=False,
    )
```
